32 devices in a mesh: sp: 4 (over y, x), ep: 8 (over z, core).
Axes of the slice: x: 2, y: 2, z: 4, core: 2. Of those that a mesh axis runs over, the one named last changes fastest.
Arguments:
- residual: bfloat16 [4096, 4096], P(('sp', 'ep')), may hold values from -40 to 40
- queries: bfloat16 [4096, 4096], P(('sp', 'ep')), may hold values from -6 to 6
- key_rows: bfloat16 [4096, 1024], P(('sp', 'ep')), may hold values from -6 to 6
- value_rows: bfloat16 [4096, 1024], P(('sp', 'ep')), may hold values from -6 to 6
- visible: int32 [32, 5], replicated, may hold values from 0 to 1, as said below
- out_proj: bfloat16 [4096, 4096], P(('sp', 'ep')), may hold values from -0.09375 to 0.09375
- norm_gain: float32 [4096], replicated, may hold values from 0.5 to 1.5
- expert_ids: int32 [4096, 2], P(('sp', 'ep')), may hold values from 0 to 7, all different within a row; in each aligned block of 128 rows (0 to 127, 128 to 255, ...) at most 40 rows name the same one
- route_weight: float32 [4096, 2], P(('sp', 'ep')), may hold values from 0.2 to 1
- expert_gate: bfloat16 [2, 7168, 4096], P(None, 'ep'), may hold values from -0.09375 to 0.09375
- expert_up: bfloat16 [2, 7168, 4096], P(None, 'ep'), may hold values from -0.09375 to 0.09375
- expert_down: bfloat16 [2, 7168, 4096], P(None, 'ep'), may hold values from -0.0625 to 0.0625
Outputs:
- layer_out: bfloat16 [4096, 4096], P(('sp', 'ep'))
The draws below stay inside these ranges and needn't reach their ends.
Inputs may be any that keep to these rules, and one draw needn't show every extreme that they name: The sequence is packed with documents that are runs of whole blocks of 128 tokens, the first of them 5 blocks or longer; visible[q, d] is 1 exactly when block q - d exists and lies in the document of block q, so visible[q, 0] = 1. `expert_ids`: each token names two different experts. Among the 128 tokens of one block no expert is named by more than 40 tokens.
All inputs are finite; a program needn't handle non-finite values.
Results may differ from the reference program's by a relative error of at most 0.0065.
Values may be sent and summed in bfloat16 or wider, within the bound.
A program may use at most 128 MiB of HBM per device.

```python
import math
import jax
import jax.numpy as jnp
import numpy as np
from jax import lax

D = 4096
HEADS = 32
KV_HEADS = 8
HEAD = 128
EXPERTS = 8
EXP_WIN = 2
FF_WIN = 7168
TOK_DEV = 128
TOKENS = 4096
BLOCKS = 32
SPAN = 5
CAP = 40
N_SP = 4
N_EP = 8


def paired_fields(key):
    key_query, key_keys = jax.random.split(key, 2)
    query_field = jnp.clip(jax.random.normal(key_query, (TOKENS, HEADS * HEAD), jnp.float32), -6.0, 6.0)
    key_field = jnp.clip(jax.random.normal(key_keys, (TOKENS, KV_HEADS * HEAD), jnp.float32), -6.0, 6.0)
    return (query_field, key_field)


def draw_queries(key, part):
    query_field, key_field = paired_fields(jax.random.fold_in(key, 71))
    return query_field.astype(jnp.bfloat16)


def draw_key_rows(key, part):
    query_field, key_field = paired_fields(jax.random.fold_in(key, 71))
    return key_field.astype(jnp.bfloat16)


def draw_residual(key, part):
    key_base = jax.random.fold_in(jax.random.fold_in(key, 13), 0)
    base_field = jnp.clip(jax.random.normal(key_base, (TOKENS, D), jnp.float32), -4.0, 4.0)
    return base_field.astype(jnp.bfloat16)


def draw_visible(key, part):
    doc_starts = jax.random.randint(jax.random.fold_in(key, 29), (BLOCKS,), 0, 5) == 0
    block_number = jnp.arange(BLOCKS, dtype=jnp.int32)
    doc_starts = jnp.where(block_number < SPAN, block_number == 0, doc_starts)
    doc_index = jnp.cumsum(doc_starts.astype(jnp.int32))
    query_block = block_number[:, None]
    key_block = query_block - jnp.arange(SPAN, dtype=jnp.int32)[None, :]
    same_doc = doc_index[query_block] == doc_index[jnp.clip(key_block, 0, BLOCKS - 1)]
    return ((key_block >= 0) & same_doc).astype(jnp.int32)


def shard_levels(own_key, extent, pieces, least, top_value):
    gain, own = 1.0, jax.random.fold_in(own_key, 6)
    for dim, blocks in pieces:
        draws = jnp.exp(jax.random.uniform(jax.random.fold_in(own, dim), (blocks,), jnp.float32, least / len(pieces), top_value / len(pieces)))
        gain = gain * jnp.repeat(draws, extent[dim] // blocks).reshape([-1 if axis == dim else 1 for axis in range(len(extent))])
    return gain


def routed_block(stream_key, own, number, rows, amount, top, limit, lean):
    sequence = jax.random.permutation(stream_key, amount)
    heavy_load, common = shares(amount, rows * top, limit, lean, True), shares(amount, rows * top, limit, lean, False)
    places = jnp.arange(amount)

    def named(sizes, turn):
        used = int((sizes > 0).sum())
        fixed = max(1, used // 4)
        moved = fixed + (places - fixed + turn * (used - fixed)) % max(1, amount - fixed)
        return jnp.zeros((amount,), jnp.int32).at[sequence[jnp.where(places < fixed, places, moved)]].set(jnp.asarray(sizes, jnp.int32))

    sizes = jnp.where(number % 4 == 0, named(heavy_load, number // 4), named(common, number - number // 4 - 1))
    mixed = jax.random.permutation(jax.random.fold_in(own, 3), amount)
    giver, sink = mixed[0:amount // 2 * 2:2], mixed[1:amount // 2 * 2:2]
    room = jnp.minimum(sizes[giver] - 1, limit - sizes[sink]) // 2
    room = jnp.where((giver == sequence[0]) | (sink == sequence[0]) | (sizes[sink] == 0), 0, jnp.maximum(room, 0))
    moved = jax.random.randint(jax.random.fold_in(own, 4), (amount // 2,), 0, 1 << 20) % (room + 1)
    sizes = sizes.at[giver].add(-moved).at[sink].add(moved)
    items = jnp.searchsorted(jnp.cumsum(sizes), jnp.arange(rows * top), side="right").astype(jnp.int32)
    listing = items.reshape(top, rows).T
    listing = listing[jax.random.permutation(jax.random.fold_in(own, 1), rows)]
    turn = jax.random.randint(jax.random.fold_in(own, 2), (rows, 1), 0, top)
    return jnp.take_along_axis(listing, (jnp.arange(top)[None, :] + turn) % top, axis=1)


def shares(count, total, limit, lean, full):
    loads = [(1 << 20) // math.isqrt(rank ** lean) + 1 for rank in range(1, count + 1)]
    largest = limit if full else min(limit, max(-(-total // count), total * loads[0] // sum(loads)))
    least = 1 if total - largest >= count - 1 else 0
    given, surplus = [largest] + [least] * (count - 1), total - largest - least * (count - 1)
    while surplus > 0:
        free = [i for i in range(1, count) if given[i] < largest] or [i for i in range(1, count) if given[i] < limit]
        pool, left = sum([loads[i] for i in free]), surplus
        for i in free:
            more = min(limit - given[i], max(1, left * loads[i] // pool), surplus)
            given[i] = given[i] + more
            surplus = surplus - more
    return np.array(given)


def noise(own_key, shape, spread, bound, pieces=(), held_as=jnp.bfloat16):
    entries = jax.random.normal(own_key, shape, jnp.float32) * spread
    if len(pieces) > 0:
        entries = shard_levels(own_key, shape, pieces, -0.22, 0.18) * entries
    return jnp.clip(entries, min=-bound, max=bound).astype(held_as)


def setup_inputs(seed: int = 0) -> dict:
    arg_keys = jax.random.split(jax.random.key(seed), 13)
    residual = draw_residual(jax.random.fold_in(arg_keys[12], 71), 0)
    queries = draw_queries(jax.random.fold_in(arg_keys[12], 71), 0)
    key_rows = draw_key_rows(jax.random.fold_in(arg_keys[12], 71), 0)
    value_rows = noise(arg_keys[3], (TOKENS, KV_HEADS * HEAD), 1.0, 6.0, ((0, 32),))
    visible = draw_visible(jax.random.fold_in(arg_keys[12], 71), 0)
    out_proj = noise(arg_keys[5], (HEADS * HEAD, D), (HEADS * HEAD) ** -0.5, 0.09375, ((0, 32),))
    norm_gain = jnp.clip(1.0 + 0.1 * jax.random.normal(arg_keys[6], (D,), jnp.float32), 0.5, 1.5)
    expert_ids_keys = jax.random.split(jax.random.fold_in(arg_keys[7], 1), TOKENS // TOK_DEV)
    expert_ids_turns = jax.random.permutation(jax.random.fold_in(arg_keys[7], 3), TOKENS // TOK_DEV)
    expert_ids = jax.vmap(lambda own, number: routed_block(jax.random.fold_in(arg_keys[7], 2), own, number, TOK_DEV, EXPERTS, 2, CAP, 2))(expert_ids_keys, expert_ids_turns).reshape((TOKENS, 2))
    route_weight = jnp.clip(0.2 + 0.8 * jax.random.uniform(arg_keys[8], (TOKENS, 2), jnp.float32) ** shard_levels(arg_keys[8], (TOKENS, 2), ((0, 32),), -0.2, 0.2), 0.2, 1.0)
    expert_gate = noise(arg_keys[9], (EXP_WIN, FF_WIN, D), D ** -0.5, 0.09375, ((1, 8),))
    expert_up = noise(arg_keys[10], (EXP_WIN, FF_WIN, D), D ** -0.5, 0.09375, ((1, 8),))
    expert_down = noise(arg_keys[11], (EXP_WIN, FF_WIN, D), FF_WIN ** -0.5, 0.0625, ((1, 8),))
    return dict(residual=residual, queries=queries, key_rows=key_rows, value_rows=value_rows, visible=visible, out_proj=out_proj, norm_gain=norm_gain, expert_ids=expert_ids, route_weight=route_weight, expert_gate=expert_gate, expert_up=expert_up, expert_down=expert_down)


def attend_block(block_index, queries, key_padded, value_padded, visible):
    grouping = HEADS // KV_HEADS
    start_row = (block_index * TOK_DEV).astype(jnp.int32)
    query_block = lax.dynamic_slice_in_dim(queries, start_row, TOK_DEV, 0).astype(jnp.float32)
    query_block = query_block.reshape(TOK_DEV, KV_HEADS, grouping, HEAD)
    key_block = lax.dynamic_slice_in_dim(key_padded, start_row, SPAN * TOK_DEV, 0)
    key_block = key_block.reshape(SPAN, TOK_DEV, KV_HEADS, HEAD)[::-1]
    value_block = lax.dynamic_slice_in_dim(value_padded, start_row, SPAN * TOK_DEV, 0)
    value_block = value_block.reshape(SPAN, TOK_DEV, KV_HEADS, HEAD)[::-1]
    scores = jnp.einsum('tgrh,dugh->grtdu', query_block, key_block) * (1.0 / math.sqrt(HEAD))
    seen = lax.dynamic_index_in_dim(visible, block_index, 0, keepdims=False)
    position = jnp.arange(TOK_DEV)
    distances = jnp.arange(SPAN)
    allowed = (seen[None, :, None] > 0) & ((distances[None, :, None] > 0) | (position[None, None, :] <= position[:, None, None]))
    scores = jnp.where(allowed, scores, -1e+30)
    peak = lax.optimization_barrier(jnp.max(scores, axis=(3, 4), keepdims=True))
    weights_f = jnp.where(allowed, jnp.exp(scores - peak), 0.0)
    totals = lax.optimization_barrier(jnp.sum(weights_f, axis=(3, 4)))
    weights_b = lax.optimization_barrier(weights_f.astype(jnp.bfloat16)).astype(jnp.float32)
    summed = jnp.einsum('grtdu,dugh->tgrh', weights_b, value_block)
    summed = summed / jnp.transpose(totals, (2, 0, 1))[..., None]
    return summed.astype(jnp.bfloat16).reshape(TOK_DEV, HEADS * HEAD)

def expert_block(normed_rows, chosen_ids, chosen_weight, expert_gate, expert_up, down_table):
    slice_width = FF_WIN // N_EP
    mixture = jnp.zeros((TOK_DEV, D), jnp.float32)
    for window_index in range(EXP_WIN):
        choose = chosen_ids == window_index
        member = jnp.any(choose, axis=1)
        token_weight = lax.optimization_barrier(jnp.sum(jnp.where(choose, chosen_weight, 0.0), axis=1))
        ranked = jnp.cumsum(member.astype(jnp.int32)) - member.astype(jnp.int32)
        slot_hit = (ranked[None, :] == jnp.arange(CAP, dtype=jnp.int32)[:, None]) & member[None, :]
        picked = jnp.dot(slot_hit.astype(jnp.bfloat16), normed_rows, preferred_element_type=jnp.float32).astype(jnp.bfloat16)
        gate_act = jnp.dot(picked, expert_gate[window_index].T, preferred_element_type=jnp.float32)
        up_act = jnp.dot(picked, expert_up[window_index].T, preferred_element_type=jnp.float32)
        activated = (jax.nn.silu(gate_act) * up_act).astype(jnp.bfloat16)
        slices = jnp.einsum('cje,jed->cjd', activated.astype(jnp.float32).reshape(CAP, N_EP, slice_width), down_table[window_index])
        slot_out = lax.optimization_barrier(jnp.sum(lax.optimization_barrier(slices.astype(jnp.bfloat16)).astype(jnp.float32), axis=1))
        combine = jnp.where(slot_hit, token_weight[None, :], 0.0)
        mixture = mixture + jnp.dot(combine.T, slot_out, precision=lax.Precision.HIGHEST)
    return mixture

def reference(residual, queries, key_rows, value_rows, visible, out_proj, norm_gain, expert_ids, route_weight, expert_gate, expert_up, expert_down):
    padding = (SPAN - 1) * TOK_DEV
    key_padded = jnp.pad(key_rows.astype(jnp.float32), ((padding, 0), (0, 0)))
    value_padded = jnp.pad(value_rows.astype(jnp.float32), ((padding, 0), (0, 0)))

    def one_block(block_index):
        return attend_block(block_index, queries, key_padded, value_padded, visible)
    attended = lax.map(one_block, jnp.arange(BLOCKS, dtype=jnp.int32)).reshape(TOKENS, HEADS * HEAD)
    group_width = HEADS * HEAD // N_SP
    projected = jnp.zeros((TOKENS, D), jnp.float32)
    for group_index in range(N_SP):
        lower = group_index * group_width
        upper = lower + group_width
        part = jnp.dot(attended[:, lower:upper], out_proj[lower:upper], preferred_element_type=jnp.float32)
        projected = projected + lax.optimization_barrier(part.astype(jnp.bfloat16)).astype(jnp.float32)
    hidden_sum = residual.astype(jnp.float32) + projected
    mean_square = lax.optimization_barrier(jnp.mean(hidden_sum * hidden_sum, axis=-1, keepdims=True))
    normed = (hidden_sum * lax.rsqrt(mean_square + 1e-05) * norm_gain).astype(jnp.bfloat16)
    down_table = expert_down.astype(jnp.float32).reshape(EXP_WIN, N_EP, FF_WIN // N_EP, D)

    def moe_block(packed):
        normed_rows, chosen_ids, chosen_weight = packed
        return expert_block(normed_rows, chosen_ids, chosen_weight, expert_gate, expert_up, down_table)
    expert_mix = lax.map(moe_block, (normed.reshape(BLOCKS, TOK_DEV, D), expert_ids.reshape(BLOCKS, TOK_DEV, 2), route_weight.reshape(BLOCKS, TOK_DEV, 2)))
    expert_mix = expert_mix.reshape(TOKENS, D)
    return (hidden_sum + expert_mix).astype(jnp.bfloat16)
```

```python
import functools
import math

import jax
import jax.numpy as jnp
from jax import lax
from jax.experimental import pallas as pl
from jax.experimental.pallas import tpu as pltpu
from jax.sharding import PartitionSpec as P

HEAD = 128
CAP = 40


def attend(reach, grouping, seen_ref, q_ref, *refs):
    keys, values, out_ref = refs[:reach], refs[reach : 2 * reach], refs[2 * reach]
    tokens = q_ref.shape[0]
    rows = grouping * tokens
    query = jnp.concatenate([q_ref[:, r * HEAD : (r + 1) * HEAD] for r in range(grouping)], axis=0)
    row = lax.broadcasted_iota(jnp.int32, (rows, tokens), 0) % tokens
    column = lax.broadcasted_iota(jnp.int32, (rows, tokens), 1)
    scores = []
    for d in range(reach):
        score = lax.dot_general(
            query, keys[d][...], (((1,), (1,)), ((), ())), preferred_element_type=jnp.float32
        ) * (1.0 / math.sqrt(HEAD))
        if d == 0:
            score = jnp.where(column <= row, score, -1e30)
        else:
            score = jnp.where(seen_ref[0, d] > 0, score, -1e30)
        scores.append(score)
    peak = functools.reduce(jnp.maximum, scores)
    peak = jnp.max(peak, axis=1, keepdims=True)
    total = jnp.zeros((rows, tokens), jnp.float32)
    summed = jnp.zeros((rows, HEAD), jnp.float32)
    for d in range(reach):
        weight = jnp.exp(scores[d] - peak)
        total = total + weight
        summed = summed + jnp.dot(
            weight.astype(jnp.bfloat16), values[d][...], preferred_element_type=jnp.float32
        )
    summed = (summed / jnp.sum(total, axis=1, keepdims=True)).astype(jnp.bfloat16)
    for r in range(grouping):
        out_ref[0, :, r * HEAD : (r + 1) * HEAD] = summed[r * tokens : (r + 1) * tokens]


def attention(queries, windows, seen, sp_count):
    tokens, width = queries.shape
    reach = len(windows)
    key_heads = windows[0].shape[1] // (2 * HEAD)
    grouping = width // (key_heads * HEAD)
    per_group = key_heads // sp_count
    block = lambda offset: pl.BlockSpec((tokens, HEAD), lambda h: (0, offset + h))
    return pl.pallas_call(
        functools.partial(attend, reach, grouping),
        grid=(key_heads,),
        out_shape=jax.ShapeDtypeStruct((sp_count, tokens, width // sp_count), jnp.bfloat16),
        in_specs=[
            pl.BlockSpec(memory_space=pltpu.SMEM),
            pl.BlockSpec((tokens, grouping * HEAD), lambda h: (0, h)),
        ]
        + [block(0)] * reach
        + [block(key_heads)] * reach,
        out_specs=pl.BlockSpec(
            (1, tokens, grouping * HEAD), lambda h: (h // per_group, 0, h % per_group)
        ),
        compiler_params=pltpu.CompilerParams(dimension_semantics=("arbitrary",)),
        cost_estimate=pl.CostEstimate(
            flops=4 * tokens * tokens * reach * width,
            bytes_accessed=4 * tokens * width + 4 * reach * tokens * key_heads * HEAD,
            transcendentals=tokens * tokens * reach * key_heads * grouping,
        ),
        name="attend",
    )(seen, queries, *windows, *windows)


def key_windows(own, reach, sp_count, ep_count, parity):
    axes = ("sp", "ep")
    blocks = sp_count * ep_count
    ahead = [(b, b + 2) for b in range(blocks - 2)]
    swap = [(b, b ^ 1) for b in range(blocks)]
    even = [own]
    for _ in range((reach - 1) // 2):
        even.append(lax.ppermute(even[-1], axes, ahead))
    windows = [own]
    for j in range((reach - 1) // 2):
        windows.append(
            lax.ppermute(jnp.where(parity == 0, even[j], even[j + 1]), axes, swap)
        )
        windows.append(even[j + 1])
    return windows


def local(
    residual,
    queries,
    key_rows,
    value_rows,
    visible,
    out_proj,
    norm_gain,
    expert_ids,
    route_weight,
    expert_gate,
    expert_up,
    expert_down,
):
    sp_count = lax.axis_size("sp")
    ep_count = lax.axis_size("ep")
    ep_index = lax.axis_index("ep")
    block_index = lax.axis_index("sp") * ep_count + ep_index
    tokens = residual.shape[0]
    reach = visible.shape[1]
    proj_full = lax.all_gather(out_proj, "ep", axis=0, tiled=True)
    own = jnp.concatenate([key_rows, value_rows], axis=1)
    windows = key_windows(own, reach, sp_count, ep_count, ep_index % 2)
    seen = lax.dynamic_slice_in_dim(visible, block_index, 1, 0)
    attended = attention(queries, windows, seen, sp_count)
    attended = lax.all_to_all(attended, "sp", split_axis=0, concat_axis=0, tiled=True)
    attended = attended.reshape(sp_count * tokens, attended.shape[2])
    projected = lax.psum_scatter(
        jnp.dot(attended, proj_full, preferred_element_type=jnp.float32).astype(jnp.bfloat16),
        "sp",
        scatter_dimension=0,
        tiled=True,
    ).astype(jnp.float32)
    hidden_sum = residual.astype(jnp.float32) + projected
    mean_square = jnp.mean(hidden_sum * hidden_sum, axis=-1, keepdims=True)
    normed = (hidden_sum * lax.rsqrt(mean_square + 1e-05) * norm_gain).astype(jnp.bfloat16)
    window_experts = expert_gate.shape[0]
    capacity = CAP
    choose = expert_ids[None] == jnp.arange(window_experts, dtype=jnp.int32)[:, None, None]
    member = jnp.any(choose, axis=2)
    token_weight = jnp.sum(jnp.where(choose, route_weight[None], 0.0), axis=2)
    earlier = jnp.tril(jnp.ones((tokens, tokens), jnp.float32), -1)
    ranked = jnp.sum(jnp.where(member[:, None, :], earlier[None], 0.0), axis=2).astype(jnp.int32)
    slot_hit = (
        ranked[:, None, :] == jnp.arange(capacity, dtype=jnp.int32)[None, :, None]
    ) & member[:, None, :]
    dispatch = slot_hit.astype(jnp.bfloat16)
    combine = jnp.where(slot_hit, token_weight[:, None, :], 0.0)
    pieces = [
        lax.all_gather(
            jnp.dot(dispatch[w], normed, preferred_element_type=jnp.float32).astype(jnp.bfloat16),
            "ep",
            axis=0,
            tiled=True,
        )
        for w in range(window_experts)
    ]
    mixture = hidden_sum
    contract = (((1,), (1,)), ((), ()))
    for w in range(window_experts):
        gate_act = lax.dot_general(
            pieces[w], expert_gate[w], contract, preferred_element_type=jnp.float32
        )
        up_act = lax.dot_general(
            pieces[w], expert_up[w], contract, preferred_element_type=jnp.float32
        )
        activated = (jax.nn.silu(gate_act) * up_act).astype(jnp.bfloat16)
        partial_value = jnp.dot(activated, expert_down[w], preferred_element_type=jnp.float32)
        returned = lax.psum_scatter(
            partial_value.astype(jnp.bfloat16), "ep", scatter_dimension=0, tiled=True
        ).astype(jnp.float32)
        mixture = mixture + jnp.dot(combine[w].T, returned, precision=lax.Precision.HIGHEST)
    return mixture.astype(jnp.bfloat16)


def solution(mesh):
    rows = P(("sp", "ep"), None)
    hidden = P(None, "ep", None)
    return jax.shard_map(
        local,
        mesh=mesh,
        in_specs=(rows, rows, rows, rows, P(), rows, P(), rows, rows, hidden, hidden, hidden),
        out_specs=rows,
        check_vma=False,
    )
```

```python
import functools
import math

import jax
import jax.numpy as jnp
from jax import lax
from jax.experimental import pallas as pl
from jax.experimental.pallas import tpu as pltpu
from jax.sharding import PartitionSpec as P

HEAD = 128
CAP = 40


def attend(reach, grouping, seen_ref, q_ref, *refs):
    keys, values, out_ref = refs[:reach], refs[reach : 2 * reach], refs[2 * reach]
    tokens = q_ref.shape[0]
    rows = grouping * tokens
    query = jnp.concatenate([q_ref[:, r * HEAD : (r + 1) * HEAD] for r in range(grouping)], axis=0)
    row = lax.broadcasted_iota(jnp.int32, (rows, tokens), 0) % tokens
    column = lax.broadcasted_iota(jnp.int32, (rows, tokens), 1)
    scores = []
    for d in range(reach):
        score = lax.dot_general(
            query, keys[d][...], (((1,), (1,)), ((), ())), preferred_element_type=jnp.float32
        ) * (1.0 / math.sqrt(HEAD))
        if d == 0:
            score = jnp.where(column <= row, score, -1e30)
        else:
            score = jnp.where(seen_ref[0, d] > 0, score, -1e30)
        scores.append(score)
    peak = functools.reduce(jnp.maximum, scores)
    peak = jnp.max(peak, axis=1, keepdims=True)
    total = jnp.zeros((rows, tokens), jnp.float32)
    summed = jnp.zeros((rows, HEAD), jnp.float32)
    for d in range(reach):
        weight = jnp.exp(scores[d] - peak)
        total = total + weight
        summed = summed + jnp.dot(
            weight.astype(jnp.bfloat16), values[d][...], preferred_element_type=jnp.float32
        )
    summed = (summed / jnp.sum(total, axis=1, keepdims=True)).astype(jnp.bfloat16)
    for r in range(grouping):
        out_ref[0, :, r * HEAD : (r + 1) * HEAD] = summed[r * tokens : (r + 1) * tokens]


def attention(queries, windows, seen, sp_count):
    tokens, width = queries.shape
    reach = len(windows)
    key_heads = windows[0].shape[1] // (2 * HEAD)
    grouping = width // (key_heads * HEAD)
    per_group = key_heads // sp_count
    block = lambda offset: pl.BlockSpec((tokens, HEAD), lambda h: (0, offset + h))
    return pl.pallas_call(
        functools.partial(attend, reach, grouping),
        grid=(key_heads,),
        out_shape=jax.ShapeDtypeStruct((sp_count, tokens, width // sp_count), jnp.bfloat16),
        in_specs=[
            pl.BlockSpec(memory_space=pltpu.SMEM),
            pl.BlockSpec((tokens, grouping * HEAD), lambda h: (0, h)),
        ]
        + [block(0)] * reach
        + [block(key_heads)] * reach,
        out_specs=pl.BlockSpec(
            (1, tokens, grouping * HEAD), lambda h: (h // per_group, 0, h % per_group)
        ),
        compiler_params=pltpu.CompilerParams(dimension_semantics=("arbitrary",)),
        cost_estimate=pl.CostEstimate(
            flops=4 * tokens * tokens * reach * width,
            bytes_accessed=4 * tokens * width + 4 * reach * tokens * key_heads * HEAD,
            transcendentals=tokens * tokens * reach * key_heads * grouping,
        ),
        name="attend",
    )(seen, queries, *windows, *windows)


def key_windows(own, reach, sp_count, ep_count, parity):
    axes = ("sp", "ep")
    blocks = sp_count * ep_count
    ahead = [(b, b + 2) for b in range(blocks - 2)]
    swap = [(b, b ^ 1) for b in range(blocks)]
    even = [own]
    for _ in range((reach - 1) // 2):
        even.append(lax.ppermute(even[-1], axes, ahead))
    windows = [own]
    for j in range((reach - 1) // 2):
        windows.append(
            lax.ppermute(jnp.where(parity == 0, even[j], even[j + 1]), axes, swap)
        )
        windows.append(even[j + 1])
    return windows


def rings(ep_count):
    right = [(e, (e + 2) % ep_count) for e in range(ep_count)]
    left = [(e, (e - 2) % ep_count) for e in range(ep_count)]
    swap = [(e, e ^ 1) for e in range(ep_count)]
    return right, left, swap


def chunk_offsets(ep_count):
    side = ep_count // 4
    return [-2 * j for j in range(side)] + [2 * j for j in range(1, side)] + [ep_count // 2]


def ring_gather(own, ep_count):
    right, left, swap = rings(ep_count)
    side = ep_count // 4
    half = own.shape[1] // 2
    to_right, to_left = [own], [own]
    for _ in range(side - 1):
        to_right.append(lax.ppermute(to_right[-1], "ep", right))
        to_left.append(lax.ppermute(to_left[-1], "ep", left))
    far = jnp.concatenate(
        [
            lax.ppermute(to_right[-1][:, :half], "ep", right),
            lax.ppermute(to_left[-1][:, half:], "ep", left),
        ],
        axis=1,
    )
    same = jnp.concatenate(to_right + to_left[1:] + [far], axis=0)
    return jnp.concatenate([same, lax.ppermute(same, "ep", swap)], axis=0)


def add(a, b):
    return (a.astype(jnp.float32) + b.astype(jnp.float32)).astype(jnp.bfloat16)


def ring_scatter(partial, ep_count):
    right, left, swap = rings(ep_count)
    side = ep_count // 4
    kept, sent = jnp.split(partial, 2, axis=0)
    chunks = jnp.split(add(kept, lax.ppermute(sent, "ep", swap)), ep_count // 2, axis=0)
    own, to_left, to_right, far = chunks[0], chunks[1:side], chunks[side:-1], chunks[-1]
    half = far.shape[1] // 2
    leftward = lax.ppermute(far[:, :half], "ep", left)
    rightward = lax.ppermute(far[:, half:], "ep", right)
    first = True
    for j in range(side - 1, 0, -1):
        down, up = to_left[j - 1], to_right[j - 1]
        if first:
            down = jnp.concatenate([add(down[:, :half], leftward), down[:, half:]], axis=1)
            up = jnp.concatenate([up[:, :half], add(up[:, half:], rightward)], axis=1)
        else:
            down, up = add(down, leftward), add(up, rightward)
        first = False
        leftward = lax.ppermute(down, "ep", left)
        rightward = lax.ppermute(up, "ep", right)
    if first:
        arrived = jnp.concatenate([leftward, rightward], axis=1).astype(jnp.float32)
    else:
        arrived = leftward.astype(jnp.float32) + rightward.astype(jnp.float32)
    return own.astype(jnp.float32) + arrived


def halving_scatter(part, bits, sp_count):
    position = lax.axis_index("sp")
    count = len(bits)
    tokens = part.shape[0] // sp_count
    part = part.reshape((2,) * count + (tokens, part.shape[1]))
    left_bits = sorted(bits, reverse=True)
    for bit in bits:
        axis = left_bits.index(bit)
        left_bits.remove(bit)
        mine = (position // (1 << bit)) % 2
        sent = lax.dynamic_index_in_dim(part, 1 - mine, axis, keepdims=False)
        kept = lax.dynamic_index_in_dim(part, mine, axis, keepdims=False)
        arrived = lax.ppermute(sent, "sp", [(s, s ^ (1 << bit)) for s in range(sp_count)])
        part = kept.astype(jnp.float32) + arrived.astype(jnp.float32)
        if left_bits:
            part = part.astype(jnp.bfloat16)
    return part


def local(
    residual,
    queries,
    key_rows,
    value_rows,
    visible,
    out_proj,
    norm_gain,
    expert_ids,
    route_weight,
    expert_gate,
    expert_up,
    expert_down,
):
    sp_count = lax.axis_size("sp")
    ep_count = lax.axis_size("ep")
    ep_index = lax.axis_index("ep")
    block_index = lax.axis_index("sp") * ep_count + ep_index
    tokens = residual.shape[0]
    reach = visible.shape[1]
    proj_full = ring_gather(out_proj, ep_count)
    own = jnp.concatenate([key_rows, value_rows], axis=1)
    windows = key_windows(own, reach, sp_count, ep_count, ep_index % 2)
    seen = lax.dynamic_slice_in_dim(visible, block_index, 1, 0)
    attended = attention(queries, windows, seen, sp_count)
    attended = lax.all_to_all(attended, "sp", split_axis=0, concat_axis=0, tiled=True)
    attended = attended.reshape(sp_count * tokens, attended.shape[2])
    heads = [(ep_index + offset) % ep_count for offset in chunk_offsets(ep_count)]
    heads += [(ep_index + 1 - 2 * (ep_index % 2) + offset) % ep_count for offset in chunk_offsets(ep_count)]
    depth = out_proj.shape[0]
    attended = jnp.concatenate(
        [lax.dynamic_slice_in_dim(attended, head * depth, depth, 1) for head in heads], axis=1
    )
    bits = list(range(sp_count.bit_length() - 1))
    half = proj_full.shape[1] // 2
    projected = jnp.concatenate(
        [
            halving_scatter(
                jnp.dot(attended, columns, preferred_element_type=jnp.float32).astype(jnp.bfloat16),
                order,
                sp_count,
            )
            for columns, order in (
                (proj_full[:, :half], bits),
                (proj_full[:, half:], bits[::-1]),
            )
        ],
        axis=1,
    )
    hidden_sum = residual.astype(jnp.float32) + projected
    mean_square = jnp.mean(hidden_sum * hidden_sum, axis=-1, keepdims=True)
    normed = (hidden_sum * lax.rsqrt(mean_square + 1e-05) * norm_gain).astype(jnp.bfloat16)
    window_experts = expert_gate.shape[0]
    capacity = CAP
    choose = expert_ids[None] == jnp.arange(window_experts, dtype=jnp.int32)[:, None, None]
    member = jnp.any(choose, axis=2)
    token_weight = jnp.sum(jnp.where(choose, route_weight[None], 0.0), axis=2)
    earlier = jnp.tril(jnp.ones((tokens, tokens), jnp.float32), -1)
    ranked = jnp.sum(jnp.where(member[:, None, :], earlier[None], 0.0), axis=2).astype(jnp.int32)
    slot_hit = (
        ranked[:, None, :] == jnp.arange(capacity, dtype=jnp.int32)[None, :, None]
    ) & member[:, None, :]
    dispatch = slot_hit.astype(jnp.bfloat16)
    combine = jnp.where(slot_hit, token_weight[:, None, :], 0.0)
    pieces = [
        ring_gather(
            jnp.dot(dispatch[w], normed, preferred_element_type=jnp.float32).astype(jnp.bfloat16),
            ep_count,
        )
        for w in range(window_experts)
    ]
    mixture = hidden_sum
    contract = (((1,), (1,)), ((), ()))
    for w in range(window_experts):
        gate_act = lax.dot_general(
            pieces[w], expert_gate[w], contract, preferred_element_type=jnp.float32
        )
        up_act = lax.dot_general(
            pieces[w], expert_up[w], contract, preferred_element_type=jnp.float32
        )
        activated = (jax.nn.silu(gate_act) * up_act).astype(jnp.bfloat16)
        partial_value = jnp.dot(activated, expert_down[w], preferred_element_type=jnp.float32)
        returned = ring_scatter(partial_value.astype(jnp.bfloat16), ep_count)
        mixture = mixture + jnp.dot(combine[w].T, returned, precision=lax.Precision.HIGHEST)
    return mixture.astype(jnp.bfloat16)


def solution(mesh):
    rows = P(("sp", "ep"), None)
    hidden = P(None, "ep", None)
    return jax.shard_map(
        local,
        mesh=mesh,
        in_specs=(rows, rows, rows, rows, P(), rows, P(), rows, rows, hidden, hidden, hidden),
        out_specs=rows,
        check_vma=False,
    )
```

```python
import functools
import math

import jax
import jax.numpy as jnp
from jax import lax
from jax.experimental import pallas as pl
from jax.experimental.pallas import tpu as pltpu
from jax.sharding import PartitionSpec as P

HEAD = 128
CAP = 40


def attend(reach, grouping, seen_ref, q_ref, *refs):
    keys, values, out_ref = refs[:reach], refs[reach : 2 * reach], refs[2 * reach]
    tokens = q_ref.shape[0]
    rows = grouping * tokens
    query = jnp.concatenate([q_ref[:, r * HEAD : (r + 1) * HEAD] for r in range(grouping)], axis=0)
    row = lax.broadcasted_iota(jnp.int32, (rows, tokens), 0) % tokens
    column = lax.broadcasted_iota(jnp.int32, (rows, tokens), 1)
    scores = []
    for d in range(reach):
        score = lax.dot_general(
            query, keys[d][...], (((1,), (1,)), ((), ())), preferred_element_type=jnp.float32
        ) * (1.0 / math.sqrt(HEAD))
        if d == 0:
            score = jnp.where(column <= row, score, -1e30)
        else:
            score = jnp.where(seen_ref[0, d] > 0, score, -1e30)
        scores.append(score)
    peak = functools.reduce(jnp.maximum, scores)
    peak = jnp.max(peak, axis=1, keepdims=True)
    total = jnp.zeros((rows, tokens), jnp.float32)
    summed = jnp.zeros((rows, HEAD), jnp.float32)
    for d in range(reach):
        weight = jnp.exp(scores[d] - peak)
        total = total + weight
        summed = summed + jnp.dot(
            weight.astype(jnp.bfloat16), values[d][...], preferred_element_type=jnp.float32
        )
    summed = (summed / jnp.sum(total, axis=1, keepdims=True)).astype(jnp.bfloat16)
    for r in range(grouping):
        out_ref[0, :, r * HEAD : (r + 1) * HEAD] = summed[r * tokens : (r + 1) * tokens]


def attention(queries, windows, seen, sp_count):
    tokens, width = queries.shape
    reach = len(windows)
    key_heads = windows[0].shape[1] // (2 * HEAD)
    grouping = width // (key_heads * HEAD)
    per_group = key_heads // sp_count
    block = lambda offset: pl.BlockSpec((tokens, HEAD), lambda h: (0, offset + h))
    return pl.pallas_call(
        functools.partial(attend, reach, grouping),
        grid=(key_heads,),
        out_shape=jax.ShapeDtypeStruct((sp_count, tokens, width // sp_count), jnp.bfloat16),
        in_specs=[
            pl.BlockSpec(memory_space=pltpu.SMEM),
            pl.BlockSpec((tokens, grouping * HEAD), lambda h: (0, h)),
        ]
        + [block(0)] * reach
        + [block(key_heads)] * reach,
        out_specs=pl.BlockSpec(
            (1, tokens, grouping * HEAD), lambda h: (h // per_group, 0, h % per_group)
        ),
        compiler_params=pltpu.CompilerParams(dimension_semantics=("arbitrary",)),
        cost_estimate=pl.CostEstimate(
            flops=4 * tokens * tokens * reach * width,
            bytes_accessed=4 * tokens * width + 4 * reach * tokens * key_heads * HEAD,
            transcendentals=tokens * tokens * reach * key_heads * grouping,
        ),
        name="attend",
    )(seen, queries, *windows, *windows)


def key_windows(own, reach, sp_count, ep_count, parity):
    axes = ("sp", "ep")
    blocks = sp_count * ep_count
    ahead = [(b, b + 2) for b in range(blocks - 2)]
    swap = [(b, b ^ 1) for b in range(blocks)]
    even = [own]
    for _ in range((reach - 1) // 2):
        even.append(lax.ppermute(even[-1], axes, ahead))
    windows = [own]
    for j in range((reach - 1) // 2):
        windows.append(
            lax.ppermute(jnp.where(parity == 0, even[j], even[j + 1]), axes, swap)
        )
        windows.append(even[j + 1])
    return windows


def rings(ep_count):
    right = [(e, (e + 2) % ep_count) for e in range(ep_count)]
    left = [(e, (e - 2) % ep_count) for e in range(ep_count)]
    swap = [(e, e ^ 1) for e in range(ep_count)]
    return right, left, swap


def ring_gather(own, ep_count):
    right, left, swap = rings(ep_count)
    side = ep_count // 4
    half = own.shape[1] // 2
    to_right, to_left = [own], [own]
    for _ in range(side - 1):
        to_right.append(lax.ppermute(to_right[-1], "ep", right))
        to_left.append(lax.ppermute(to_left[-1], "ep", left))
    far = jnp.concatenate(
        [
            lax.ppermute(to_right[-1][:, :half], "ep", right),
            lax.ppermute(to_left[-1][:, half:], "ep", left),
        ],
        axis=1,
    )
    same = jnp.concatenate(to_right + to_left[1:] + [far], axis=0)
    return jnp.concatenate([same, lax.ppermute(same, "ep", swap)], axis=0)


def add(a, b):
    return (a.astype(jnp.float32) + b.astype(jnp.float32)).astype(jnp.bfloat16)


def ring_scatter(partial, ep_count):
    right, left, swap = rings(ep_count)
    side = ep_count // 4
    kept, sent = jnp.split(partial, 2, axis=0)
    chunks = jnp.split(add(kept, lax.ppermute(sent, "ep", swap)), ep_count // 2, axis=0)
    own, to_left, to_right, far = chunks[0], chunks[1:side], chunks[side:-1], chunks[-1]
    half = far.shape[1] // 2
    leftward = lax.ppermute(far[:, :half], "ep", left)
    rightward = lax.ppermute(far[:, half:], "ep", right)
    first = True
    for j in range(side - 1, 0, -1):
        down, up = to_left[j - 1], to_right[j - 1]
        if first:
            down = jnp.concatenate([add(down[:, :half], leftward), down[:, half:]], axis=1)
            up = jnp.concatenate([up[:, :half], add(up[:, half:], rightward)], axis=1)
        else:
            down, up = add(down, leftward), add(up, rightward)
        first = False
        leftward = lax.ppermute(down, "ep", left)
        rightward = lax.ppermute(up, "ep", right)
    if first:
        arrived = jnp.concatenate([leftward, rightward], axis=1).astype(jnp.float32)
    else:
        arrived = leftward.astype(jnp.float32) + rightward.astype(jnp.float32)
    return own.astype(jnp.float32) + arrived


def halving_scatter(part, bits, sp_count):
    position = lax.axis_index("sp")
    count = len(bits)
    tokens = part.shape[0] // sp_count
    part = part.reshape((2,) * count + (tokens, part.shape[1]))
    left_bits = sorted(bits, reverse=True)
    for bit in bits:
        axis = left_bits.index(bit)
        left_bits.remove(bit)
        mine = (position // (1 << bit)) % 2
        sent = lax.dynamic_index_in_dim(part, 1 - mine, axis, keepdims=False)
        kept = lax.dynamic_index_in_dim(part, mine, axis, keepdims=False)
        arrived = lax.ppermute(sent, "sp", [(s, s ^ (1 << bit)) for s in range(sp_count)])
        part = kept.astype(jnp.float32) + arrived.astype(jnp.float32)
        if left_bits:
            part = part.astype(jnp.bfloat16)
    return part


def local(
    residual,
    queries,
    key_rows,
    value_rows,
    visible,
    out_proj,
    norm_gain,
    expert_ids,
    route_weight,
    expert_gate,
    expert_up,
    expert_down,
):
    sp_count = lax.axis_size("sp")
    ep_count = lax.axis_size("ep")
    ep_index = lax.axis_index("ep")
    block_index = lax.axis_index("sp") * ep_count + ep_index
    tokens = residual.shape[0]
    reach = visible.shape[1]
    proj_full = lax.all_gather(out_proj, "ep", axis=0, tiled=True)
    own = jnp.concatenate([key_rows, value_rows], axis=1)
    windows = key_windows(own, reach, sp_count, ep_count, ep_index % 2)
    seen = lax.dynamic_slice_in_dim(visible, block_index, 1, 0)
    attended = attention(queries, windows, seen, sp_count)
    attended = lax.all_to_all(attended, "sp", split_axis=0, concat_axis=0, tiled=True)
    attended = attended.reshape(sp_count * tokens, attended.shape[2])
    bits = list(range(sp_count.bit_length() - 1))
    half = proj_full.shape[1] // 2
    projected = jnp.concatenate(
        [
            halving_scatter(
                jnp.dot(attended, columns, preferred_element_type=jnp.float32).astype(jnp.bfloat16),
                order,
                sp_count,
            )
            for columns, order in (
                (proj_full[:, :half], bits),
                (proj_full[:, half:], bits[::-1]),
            )
        ],
        axis=1,
    )
    hidden_sum = residual.astype(jnp.float32) + projected
    mean_square = jnp.mean(hidden_sum * hidden_sum, axis=-1, keepdims=True)
    normed = (hidden_sum * lax.rsqrt(mean_square + 1e-05) * norm_gain).astype(jnp.bfloat16)
    window_experts = expert_gate.shape[0]
    capacity = CAP
    choose = expert_ids[None] == jnp.arange(window_experts, dtype=jnp.int32)[:, None, None]
    member = jnp.any(choose, axis=2)
    token_weight = jnp.sum(jnp.where(choose, route_weight[None], 0.0), axis=2)
    earlier = jnp.tril(jnp.ones((tokens, tokens), jnp.float32), -1)
    ranked = jnp.sum(jnp.where(member[:, None, :], earlier[None], 0.0), axis=2).astype(jnp.int32)
    slot_hit = (
        ranked[:, None, :] == jnp.arange(capacity, dtype=jnp.int32)[None, :, None]
    ) & member[:, None, :]
    dispatch = slot_hit.astype(jnp.bfloat16)
    combine = jnp.where(slot_hit, token_weight[:, None, :], 0.0)
    outgoing = [
        jnp.dot(dispatch[w], normed, preferred_element_type=jnp.float32).astype(jnp.bfloat16)
        for w in range(window_experts)
    ]
    pieces = [
        lax.all_gather(outgoing[w], "ep", axis=0, tiled=True)
        if w % 2 == 0
        else ring_gather(outgoing[w], ep_count)
        for w in range(window_experts)
    ]
    mixture = hidden_sum
    contract = (((1,), (1,)), ((), ()))
    for w in range(window_experts):
        gate_act = lax.dot_general(
            pieces[w], expert_gate[w], contract, preferred_element_type=jnp.float32
        )
        up_act = lax.dot_general(
            pieces[w], expert_up[w], contract, preferred_element_type=jnp.float32
        )
        activated = (jax.nn.silu(gate_act) * up_act).astype(jnp.bfloat16)
        partial_value = jnp.dot(activated, expert_down[w], preferred_element_type=jnp.float32)
        partial_value = partial_value.astype(jnp.bfloat16)
        if w % 2 == 0:
            returned = lax.psum_scatter(
                partial_value, "ep", scatter_dimension=0, tiled=True
            ).astype(jnp.float32)
        else:
            returned = ring_scatter(partial_value, ep_count)
        mixture = mixture + jnp.dot(combine[w].T, returned, precision=lax.Precision.HIGHEST)
    return mixture.astype(jnp.bfloat16)


def solution(mesh):
    rows = P(("sp", "ep"), None)
    hidden = P(None, "ep", None)
    return jax.shard_map(
        local,
        mesh=mesh,
        in_specs=(rows, rows, rows, rows, P(), rows, P(), rows, rows, hidden, hidden, hidden),
        out_specs=rows,
        check_vma=False,
    )
```

```python
import functools
import math

import jax
import jax.numpy as jnp
from jax import lax
from jax.experimental import pallas as pl
from jax.experimental.pallas import tpu as pltpu
from jax.sharding import PartitionSpec as P

HEAD = 128
CAP = 40


def attend(reach, grouping, seen_ref, q_ref, *refs):
    keys, values, out_ref = refs[:reach], refs[reach : 2 * reach], refs[2 * reach]
    tokens = q_ref.shape[0]
    rows = grouping * tokens
    query = jnp.concatenate([q_ref[:, r * HEAD : (r + 1) * HEAD] for r in range(grouping)], axis=0)
    row = lax.broadcasted_iota(jnp.int32, (rows, tokens), 0) % tokens
    column = lax.broadcasted_iota(jnp.int32, (rows, tokens), 1)
    scores = []
    for d in range(reach):
        score = lax.dot_general(
            query, keys[d][...], (((1,), (1,)), ((), ())), preferred_element_type=jnp.float32
        ) * (1.0 / math.sqrt(HEAD))
        if d == 0:
            score = jnp.where(column <= row, score, -1e30)
        else:
            score = jnp.where(seen_ref[0, d] > 0, score, -1e30)
        scores.append(score)
    peak = functools.reduce(jnp.maximum, scores)
    peak = jnp.max(peak, axis=1, keepdims=True)
    total = jnp.zeros((rows, tokens), jnp.float32)
    summed = jnp.zeros((rows, HEAD), jnp.float32)
    for d in range(reach):
        weight = jnp.exp(scores[d] - peak)
        total = total + weight
        summed = summed + jnp.dot(
            weight.astype(jnp.bfloat16), values[d][...], preferred_element_type=jnp.float32
        )
    summed = (summed / jnp.sum(total, axis=1, keepdims=True)).astype(jnp.bfloat16)
    for r in range(grouping):
        out_ref[0, :, r * HEAD : (r + 1) * HEAD] = summed[r * tokens : (r + 1) * tokens]


def attention(queries, windows, seen, sp_count):
    tokens, width = queries.shape
    reach = len(windows)
    key_heads = windows[0].shape[1] // (2 * HEAD)
    grouping = width // (key_heads * HEAD)
    per_group = key_heads // sp_count
    block = lambda offset: pl.BlockSpec((tokens, HEAD), lambda h: (0, offset + h))
    return pl.pallas_call(
        functools.partial(attend, reach, grouping),
        grid=(key_heads,),
        out_shape=jax.ShapeDtypeStruct((sp_count, tokens, width // sp_count), jnp.bfloat16),
        in_specs=[
            pl.BlockSpec(memory_space=pltpu.SMEM),
            pl.BlockSpec((tokens, grouping * HEAD), lambda h: (0, h)),
        ]
        + [block(0)] * reach
        + [block(key_heads)] * reach,
        out_specs=pl.BlockSpec(
            (1, tokens, grouping * HEAD), lambda h: (h // per_group, 0, h % per_group)
        ),
        compiler_params=pltpu.CompilerParams(dimension_semantics=("arbitrary",)),
        cost_estimate=pl.CostEstimate(
            flops=4 * tokens * tokens * reach * width,
            bytes_accessed=4 * tokens * width + 4 * reach * tokens * key_heads * HEAD,
            transcendentals=tokens * tokens * reach * key_heads * grouping,
        ),
        name="attend",
    )(seen, queries, *windows, *windows)


def key_windows(own, reach, sp_count, ep_count, parity):
    axes = ("sp", "ep")
    blocks = sp_count * ep_count
    ahead = [(b, b + 2) for b in range(blocks - 2)]
    swap = [(b, b ^ 1) for b in range(blocks)]
    even = [own]
    for _ in range((reach - 1) // 2):
        even.append(lax.ppermute(even[-1], axes, ahead))
    windows = [own]
    for j in range((reach - 1) // 2):
        windows.append(
            lax.ppermute(jnp.where(parity == 0, even[j], even[j + 1]), axes, swap)
        )
        windows.append(even[j + 1])
    return windows


def rings(ep_count):
    right = [(e, (e + 2) % ep_count) for e in range(ep_count)]
    left = [(e, (e - 2) % ep_count) for e in range(ep_count)]
    swap = [(e, e ^ 1) for e in range(ep_count)]
    return right, left, swap


def ring_gather(own, ep_count):
    right, left, swap = rings(ep_count)
    side = ep_count // 4
    half = own.shape[1] // 2
    to_right, to_left = [own], [own]
    for _ in range(side - 1):
        to_right.append(lax.ppermute(to_right[-1], "ep", right))
        to_left.append(lax.ppermute(to_left[-1], "ep", left))
    far = jnp.concatenate(
        [
            lax.ppermute(to_right[-1][:, :half], "ep", right),
            lax.ppermute(to_left[-1][:, half:], "ep", left),
        ],
        axis=1,
    )
    same = jnp.concatenate(to_right + to_left[1:] + [far], axis=0)
    return jnp.concatenate([same, lax.ppermute(same, "ep", swap)], axis=0)


def add(a, b):
    return (a.astype(jnp.float32) + b.astype(jnp.float32)).astype(jnp.bfloat16)


def ring_scatter(partial, ep_count):
    right, left, swap = rings(ep_count)
    side = ep_count // 4
    kept, sent = jnp.split(partial, 2, axis=0)
    chunks = jnp.split(add(kept, lax.ppermute(sent, "ep", swap)), ep_count // 2, axis=0)
    own, to_left, to_right, far = chunks[0], chunks[1:side], chunks[side:-1], chunks[-1]
    half = far.shape[1] // 2
    leftward = lax.ppermute(far[:, :half], "ep", left)
    rightward = lax.ppermute(far[:, half:], "ep", right)
    first = True
    for j in range(side - 1, 0, -1):
        down, up = to_left[j - 1], to_right[j - 1]
        if first:
            down = jnp.concatenate([add(down[:, :half], leftward), down[:, half:]], axis=1)
            up = jnp.concatenate([up[:, :half], add(up[:, half:], rightward)], axis=1)
        else:
            down, up = add(down, leftward), add(up, rightward)
        first = False
        leftward = lax.ppermute(down, "ep", left)
        rightward = lax.ppermute(up, "ep", right)
    if first:
        arrived = jnp.concatenate([leftward, rightward], axis=1).astype(jnp.float32)
    else:
        arrived = leftward.astype(jnp.float32) + rightward.astype(jnp.float32)
    return own.astype(jnp.float32) + arrived


def halving_scatter(attended, columns, bits, sp_count):
    position = lax.axis_index("sp")
    count = len(bits)
    tokens, depth = attended.shape[0] // sp_count, attended.shape[1]
    part = attended.reshape((2,) * count + (tokens, depth))
    left_bits = sorted(bits, reverse=True)
    for step, bit in enumerate(bits):
        axis = left_bits.index(bit)
        left_bits.remove(bit)
        mine = (position // (1 << bit)) % 2
        sent = lax.dynamic_index_in_dim(part, 1 - mine, axis, keepdims=False)
        kept = lax.dynamic_index_in_dim(part, mine, axis, keepdims=False)
        if step == 0:
            shape = sent.shape[:-1] + (columns.shape[1],)
            sent, kept = (
                jnp.dot(rows.reshape(-1, depth), columns, preferred_element_type=jnp.float32)
                .astype(jnp.bfloat16)
                .reshape(shape)
                for rows in (sent, kept)
            )
        arrived = lax.ppermute(sent, "sp", [(s, s ^ (1 << bit)) for s in range(sp_count)])
        part = kept.astype(jnp.float32) + arrived.astype(jnp.float32)
        if left_bits:
            part = part.astype(jnp.bfloat16)
    return part


def local(
    residual,
    queries,
    key_rows,
    value_rows,
    visible,
    out_proj,
    norm_gain,
    expert_ids,
    route_weight,
    expert_gate,
    expert_up,
    expert_down,
):
    sp_count = lax.axis_size("sp")
    ep_count = lax.axis_size("ep")
    ep_index = lax.axis_index("ep")
    block_index = lax.axis_index("sp") * ep_count + ep_index
    tokens = residual.shape[0]
    reach = visible.shape[1]
    proj_full = lax.all_gather(out_proj, "ep", axis=0, tiled=True)
    own = jnp.concatenate([key_rows, value_rows], axis=1)
    windows = key_windows(own, reach, sp_count, ep_count, ep_index % 2)
    seen = lax.dynamic_slice_in_dim(visible, block_index, 1, 0)
    attended = attention(queries, windows, seen, sp_count)
    attended = lax.all_to_all(attended, "sp", split_axis=0, concat_axis=0, tiled=True)
    attended = attended.reshape(sp_count * tokens, attended.shape[2])
    bits = list(range(sp_count.bit_length() - 1))
    half = proj_full.shape[1] // 2
    projected = jnp.concatenate(
        [
            halving_scatter(
                attended,
                columns,
                order,
                sp_count,
            )
            for columns, order in (
                (proj_full[:, :half], bits),
                (proj_full[:, half:], bits[::-1]),
            )
        ],
        axis=1,
    )
    hidden_sum = residual.astype(jnp.float32) + projected
    mean_square = jnp.mean(hidden_sum * hidden_sum, axis=-1, keepdims=True)
    normed = (hidden_sum * lax.rsqrt(mean_square + 1e-05) * norm_gain).astype(jnp.bfloat16)
    window_experts = expert_gate.shape[0]
    capacity = CAP
    choose = expert_ids[None] == jnp.arange(window_experts, dtype=jnp.int32)[:, None, None]
    member = jnp.any(choose, axis=2)
    token_weight = jnp.sum(jnp.where(choose, route_weight[None], 0.0), axis=2)
    earlier = jnp.tril(jnp.ones((tokens, tokens), jnp.float32), -1)
    ranked = jnp.sum(jnp.where(member[:, None, :], earlier[None], 0.0), axis=2).astype(jnp.int32)
    slot_hit = (
        ranked[:, None, :] == jnp.arange(capacity, dtype=jnp.int32)[None, :, None]
    ) & member[:, None, :]
    dispatch = slot_hit.astype(jnp.bfloat16)
    combine = jnp.where(slot_hit, token_weight[:, None, :], 0.0)
    outgoing = [
        jnp.dot(dispatch[w], normed, preferred_element_type=jnp.float32).astype(jnp.bfloat16)
        for w in range(window_experts)
    ]
    pieces = []
    for w in range(window_experts):
        if w % 2 == 0:
            pieces.append(lax.all_gather(outgoing[w], "ep", axis=0, tiled=True))
        else:
            later, pieces[-1] = lax.optimization_barrier((outgoing[w], pieces[-1]))
            pieces.append(ring_gather(later, ep_count))
    mixture = hidden_sum
    contract = (((1,), (1,)), ((), ()))
    for w in range(window_experts):
        gate_act = lax.dot_general(
            pieces[w], expert_gate[w], contract, preferred_element_type=jnp.float32
        )
        up_act = lax.dot_general(
            pieces[w], expert_up[w], contract, preferred_element_type=jnp.float32
        )
        activated = (jax.nn.silu(gate_act) * up_act).astype(jnp.bfloat16)
        partial_value = jnp.dot(activated, expert_down[w], preferred_element_type=jnp.float32)
        partial_value = partial_value.astype(jnp.bfloat16)
        if w % 2 == 0:
            returned = lax.psum_scatter(
                partial_value, "ep", scatter_dimension=0, tiled=True
            ).astype(jnp.float32)
        else:
            returned = ring_scatter(partial_value, ep_count)
        mixture = mixture + jnp.dot(combine[w].T, returned, precision=lax.Precision.HIGHEST)
    return mixture.astype(jnp.bfloat16)


def solution(mesh):
    rows = P(("sp", "ep"), None)
    hidden = P(None, "ep", None)
    return jax.shard_map(
        local,
        mesh=mesh,
        in_specs=(rows, rows, rows, rows, P(), rows, P(), rows, rows, hidden, hidden, hidden),
        out_specs=rows,
        check_vma=False,
    )
```
